256 devices in a mesh: gx: 64 (over z, x, core), gy: 4 (over y).
Axes of the slice: x: 4, y: 4, z: 8, core: 2. Of those that a mesh axis runs over, the one named last changes fastest.
Arguments:
- pressure: float32 [512, 512, 128], P('gx', 'gy'), may hold values from -6 to 8
- vel_y: float32 [512, 512, 128], P('gx', 'gy'), may hold values from -6 to 6
- vel_z: float32 [512, 512, 128], P('gx', 'gy'), may hold values from -6 to 6
- material: int32 [512, 512, 128], P('gx', 'gy'), may hold values from 0 to 7
- absorb_table: float32 [8], replicated, may hold values from 0.02 to 4
Outputs:
- pressure_next: float32 [512, 512, 128], P('gx', 'gy')
- vel_y_next: float32 [512, 512, 128], P('gx', 'gy')
- vel_z_next: float32 [512, 512, 128], P('gx', 'gy')
The draws below stay inside these ranges and needn't reach their ends.
All inputs are finite; a program needn't handle non-finite values.
Results may differ from the reference program's by a relative error of at most 0.0004.
Values sent between devices are 32-bit elements; how exact they have to be, the bound alone decides.
A program may use at most 128 MiB of HBM per device.

```python
import math
import jax
import jax.numpy as jnp
from jax import lax

CX = 8
NZ = 128
MATS = 8
NX = 512
NY = 512
RX = 65536


def material_order(key):
    return jax.random.permutation(jax.random.fold_in(key, 29), MATS)


def draw_absorb_table(key, part):
    order = material_order(key)
    half = MATS // 2
    spread = jax.random.uniform(jax.random.fold_in(key, 31), (MATS,), jnp.float32)
    weak = 0.02 * jnp.exp(spread * math.log(3.0))
    strong = 2.0 * jnp.exp(spread * math.log(2.0))
    ranks = jnp.arange(MATS, dtype=jnp.int32)
    values = jnp.where(ranks < half, weak, strong)
    return jnp.zeros((MATS,), jnp.float32).at[order].set(values).astype(jnp.float32)


def draw_material(key, part):
    order = material_order(key)
    half = MATS // 2
    picks = jax.random.randint(jax.random.fold_in(key, 37), (NX, NY, NZ), 0, half, dtype=jnp.int32)
    rows = jnp.arange(NX, dtype=jnp.int32)
    within = rows % CX
    blocks = rows // CX
    strong_part = within >= CX // 2
    flipped = blocks >= NX // CX // 2
    strong = jnp.logical_xor(strong_part, flipped).astype(jnp.int32)
    index = picks + half * strong[:, None, None]
    return order[index].astype(jnp.int32)


def draw_pressure(key, part):
    keys = jax.random.split(jax.random.fold_in(key, 17), 3)
    phases = jax.random.uniform(keys[0], (3,), jnp.float32, 0.0, 2.0 * math.pi)
    xs = jnp.arange(NX, dtype=jnp.float32)[:, None, None] / NX
    ys = jnp.arange(NY, dtype=jnp.float32)[None, :, None] / NY
    zs = jnp.arange(NZ, dtype=jnp.float32)[None, None, :] / NZ
    smooth = 0.2 * jnp.sin(2.0 * math.pi * xs + phases[0]) + 0.15 * jnp.cos(2.0 * math.pi * ys + phases[1]) + 0.1 * jnp.sin(2.0 * math.pi * zs + phases[2])
    block_levels = jax.random.uniform(keys[2], (NX // CX,), jnp.float32, -1.0, 1.0)
    rows = jnp.arange(NX, dtype=jnp.int32)
    blocks = rows // CX
    within = (rows % CX).astype(jnp.float32)
    steps = block_levels[blocks][:, None, None]
    orient = jnp.where(blocks < NX // CX // 2, 1.0, -1.0)
    ramp = (-1.5 * orient * (2.0 * within / (CX - 1) - 1.0))[:, None, None]
    rough = jnp.clip(jax.random.normal(keys[1], (NX, NY, NZ), jnp.float32), -2.5, 2.5)
    level = 2.0
    return (level + steps + ramp + smooth + rough).astype(jnp.float32)


def level_of(own_key, extent, pieces, smallest, high):
    factor_of, own = 1.0, jax.random.fold_in(own_key, 6)
    for dim, shards_of in pieces:
        steps = jnp.exp(jax.random.uniform(jax.random.fold_in(own, dim), (shards_of,), jnp.float32, smallest / len(pieces), high / len(pieces)))
        factor_of = factor_of * jnp.repeat(steps, extent[dim] // shards_of).reshape([-1 if axis == dim else 1 for axis in range(len(extent))])
    return factor_of


def normal_values(stream_key, extent, scale, most, pieces=(), kind=jnp.bfloat16):
    factor_of = level_of(stream_key, extent, pieces, -0.22, 0.18) if pieces else 1.0
    array = jax.random.normal(stream_key, extent, jnp.float32) * scale * factor_of
    return jnp.minimum(jnp.maximum(array, -most), most).astype(kind)


def setup_inputs(seed: int = 0) -> dict:
    seeds = jax.random.split(jax.random.key(seed), 6)
    pressure = draw_pressure(jax.random.fold_in(seeds[5], 71), 0)
    vel_y = normal_values(seeds[1], (NX, NY, NZ), 1.0, 6.0, ((0, 64), (1, 4)), jnp.float32)
    vel_z = normal_values(seeds[2], (NX, NY, NZ), 1.0, 6.0, ((0, 64), (1, 4)), jnp.float32)
    material = draw_material(jax.random.fold_in(seeds[5], 71), 0)
    absorb_table = draw_absorb_table(jax.random.fold_in(seeds[5], 71), 0)
    return {"pressure": pressure, "vel_y": vel_y, "vel_z": vel_z, "material": material, "absorb_table": absorb_table}


def reference(pressure, vel_y, vel_z, material, absorb_table):
    absorb = absorb_table[material]
    damping = 1.0 / (1.0 + absorb)
    zeros_y = jnp.zeros_like(pressure[:, :1, :])
    zeros_z = jnp.zeros_like(pressure[:, :, :1])
    upper_y = jnp.concatenate([pressure[:, 1:, :], zeros_y], axis=1)
    upper_z = jnp.concatenate([pressure[:, :, 1:], zeros_z], axis=2)
    vel_y_next = damping * (vel_y - 0.5 * (upper_y - pressure))
    vel_z_next = damping * (vel_z - 0.5 * (upper_z - pressure))
    lower_y = jnp.concatenate([zeros_y, vel_y_next[:, :-1, :]], axis=1)
    lower_z = jnp.concatenate([zeros_z, vel_z_next[:, :, :-1]], axis=2)
    source = pressure - 0.5 * (vel_y_next - lower_y + vel_z_next - lower_z)
    coupling = 1.0 * RX
    excess = (1.0 + absorb) / coupling
    scaled = source / coupling

    def forward(carry, items):
        carried, value_prev = carry
        excess_row, value_row = items
        inverse = 1.0 / (1.0 + excess_row + carried)
        value = (value_row + value_prev) * inverse
        carried_next = (excess_row + carried) * inverse
        return (carried_next, value), (inverse, value)

    start = (jnp.ones(pressure.shape[1:], jnp.float32), jnp.zeros(pressure.shape[1:], jnp.float32))
    _, (inverses, values) = lax.scan(forward, start, (excess, scaled))

    def backward(following, items):
        inverse, value = items
        current = value + inverse * following
        return current, current

    _, solved = lax.scan(backward, jnp.zeros(pressure.shape[1:], jnp.float32), (inverses, values), reverse=True)
    return solved, vel_y_next, vel_z_next
```

```python
import functools

import jax
import jax.numpy as jnp
from jax import lax
from jax.experimental import pallas as pl
from jax.experimental.pallas import tpu as pltpu
from jax.sharding import PartitionSpec as P

MATS = 8
RX = 65536
GROUP = 8
MESH = pl.DeviceIdType.MESH


def look_up(material, table):
    low = (material & 1) == 1
    mid = (material & 2) == 2
    high = material >= 4
    pairs = [jnp.where(low, table[2 * k + 1], table[2 * k]) for k in range(4)]
    quads = [jnp.where(mid, pairs[1], pairs[0]), jnp.where(mid, pairs[3], pairs[2])]
    return jnp.where(high, quads[1], quads[0])


def merge_matrix(left, right):
    ground = left[2] + right[1]
    inverse = 1.0 / (left[0] + right[0] + ground)
    to_left = left[0] * inverse
    to_right = right[0] * inverse
    joined = (to_left * right[0], left[1] + to_left * ground, right[2] + to_right * ground)
    return joined, (inverse, to_left, to_right)


def build_matrix(segments, low, high):
    if high - low == 1:
        return segments[low], None
    mid = (low + high) // 2
    left, left_tree = build_matrix(segments, low, mid)
    right, right_tree = build_matrix(segments, mid, high)
    joined, weights = merge_matrix(left, right)
    return joined, (mid - 1, weights, left_tree, right_tree)


def build_source(tree, sources, low, high, levels):
    if tree is None:
        return sources[low]
    node, (inverse, to_left, to_right), left_tree, right_tree = tree
    left = build_source(left_tree, sources, low, node + 1, levels)
    right = build_source(right_tree, sources, node + 1, high, levels)
    source = left[1] + right[0]
    levels[node] = source * inverse
    return left[0] + to_left * source, right[1] + to_right * source


def spread(tree, levels, before, after, values):
    if tree is None:
        return
    node, (_, to_left, to_right), left_tree, right_tree = tree
    value = levels[node] + to_left * before + to_right * after
    values[node] = value
    spread(left_tree, levels, before, value, values)
    spread(right_tree, levels, value, after, values)


def kernel(groups, columns, table_ref, p_hbm, vy_hbm, vz_hbm, mat_hbm, q_out, vy_out, vz_out,
           p_v, vy_v, vz_v, mat_v, vyn_v, vzn_v, r_v, a_v, tr_v, e_v, q_v,
           edge, edge_mat, halo, halo_mat,
           am_send, am_recv, as_send, as_recv, bm_send, bm_recv, bs_send, bs_recv,
           nodes_b, db_recv, nodes_a, da_recv,
           in_sem, edge_sem, out_sem, halo_send, halo_recv,
           am_ss, am_rs, as_ss, as_rs, bm_ss, bm_rs, bs_ss, bs_rs, db_ss, db_rs, da_ss, da_rs, ring_sem):
    cells, rows_y, lanes = vy_v.shape
    rows_a = rows_y // GROUP
    rows_b = rows_a // groups
    gx = lax.axis_index("gx")
    gy = lax.axis_index("gy")
    z = gx // GROUP
    a = gx % GROUP
    base = z * GROUP
    up = lax.rem(z + 1, groups) * GROUP + a
    down = lax.rem(z + groups - 1, groups) * GROUP + a
    ring = (up,) if groups == 2 else (up, down)
    has_above = gy < columns - 1
    has_below = gy > 0

    loads = [
        pltpu.make_async_copy(mat_hbm, mat_v, in_sem.at[0]),
        pltpu.make_async_copy(p_hbm, p_v.at[:, 0:rows_y, :], in_sem.at[1]),
        pltpu.make_async_copy(vy_hbm, vy_v, in_sem.at[2]),
        pltpu.make_async_copy(vz_hbm, vz_v, in_sem.at[3]),
    ]

    barrier = pltpu.get_barrier_semaphore()
    for k in range(1, GROUP):
        pl.semaphore_signal(barrier, inc=1, device_id=(base + lax.rem(a + k, GROUP), gy), device_id_type=MESH)
    for peer in ring:
        pl.semaphore_signal(barrier, inc=1, device_id=(peer, gy), device_id_type=MESH)

    @pl.when(has_above)
    def _():
        pl.semaphore_signal(barrier, inc=1, device_id=(gx, gy + 1), device_id_type=MESH)

    @pl.when(has_below)
    def _():
        pl.semaphore_signal(barrier, inc=1, device_id=(gx, gy - 1), device_id_type=MESH)

    for copy in loads:
        copy.start()
    last = pl.ds(rows_y - 1, 1)
    first = pl.ds(0, 1)
    edges = [
        pltpu.make_async_copy(mat_hbm.at[:, last, :], edge_mat, edge_sem.at[0]),
        pltpu.make_async_copy(p_hbm.at[:, last, :], edge.at[0], edge_sem.at[1]),
        pltpu.make_async_copy(vy_hbm.at[:, last, :], edge.at[1], edge_sem.at[2]),
        pltpu.make_async_copy(p_hbm.at[:, first, :], edge.at[2], edge_sem.at[3]),
    ]
    for copy in edges:
        copy.start()

    pl.semaphore_wait(barrier, GROUP - 1 + len(ring) + has_above.astype(jnp.int32) + has_below.astype(jnp.int32))

    def halo_up(k, source, target):
        return pltpu.make_async_remote_copy(
            src_ref=source, dst_ref=target, send_sem=halo_send.at[k], recv_sem=halo_recv.at[k],
            device_id=(gx, gy + 1), device_id_type=MESH)

    ups = [
        halo_up(0, mat_hbm.at[:, last, :], halo_mat),
        halo_up(1, p_hbm.at[:, last, :], halo.at[0]),
        halo_up(2, vy_hbm.at[:, last, :], halo.at[1]),
    ]
    goes_down = pltpu.make_async_remote_copy(
        src_ref=p_hbm.at[:, first, :], dst_ref=halo.at[2], send_sem=halo_send.at[3], recv_sem=halo_recv.at[3],
        device_id=(gx, gy - 1), device_id_type=MESH)

    @pl.when(has_above)
    def _():
        for copy in ups:
            copy.start()

    @pl.when(has_below)
    def _():
        goes_down.start()

    stages = groups // 2 - 1
    for stage in range(stages):
        for peer in ring:
            if stage == 0:
                pl.semaphore_signal(ring_sem.at[0], inc=1, device_id=(peer, gy), device_id_type=MESH)

    table = [table_ref[k] for k in range(MATS)]
    scale = 1.0 / RX

    loads[0].wait()
    loads[1].wait()
    loads[2].wait()
    loads[3].wait()
    row_of = lax.broadcasted_iota(jnp.int32, (rows_a, lanes), 0)
    lane_of = lax.broadcasted_iota(jnp.int32, (rows_a, lanes), 1)

    def at_rows(index, offset=0):
        return pl.ds(pl.multiple_of(index * rows_a + offset, 8), rows_a)

    def first_pass(index, matrix_ref):
        here = at_rows(index)
        after = pl.ds(pl.multiple_of(index * rows_a + rows_a, 8), 8)
        conductance = left_ground = carried = None
        for x in range(cells):
            weight = 1.0 + look_up(mat_v[x, here, :], table)
            damping = 1.0 / weight
            excess = weight * scale
            pressure = p_v[x, here, :]
            upper = pltpu.roll(pressure, rows_a - 1, axis=0)
            upper = jnp.where(row_of == rows_a - 1, p_v[x, after, :][0:1, :], upper)
            vyn_v[x, pl.ds(pl.multiple_of(index * rows_a + 8, 8), rows_a), :] = damping * (
                vy_v[x, here, :] - 0.5 * (upper - pressure))
            beyond = jnp.where(lane_of == lanes - 1, 0.0, pltpu.roll(pressure, lanes - 1, axis=1))
            vzn_v[x, here, :] = damping * (vz_v[x, here, :] - 0.5 * (beyond - pressure))
            if x == 0:
                ground = excess
                inverse = 1.0 / (2.0 + ground)
                conductance = inverse
                left_ground = conductance * ground
            elif x < cells - 1:
                ground = excess + carried
                inverse = 1.0 / (conductance + 1.0 + ground)
                conductance = conductance * inverse
                left_ground = left_ground + conductance * ground
            else:
                ground = excess + carried
            if x < cells - 1:
                carried = ground * inverse
                r_v[x, here, :] = inverse
                a_v[x, here, :] = conductance
        matrix_ref[0] = conductance
        matrix_ref[1] = left_ground
        matrix_ref[2] = ground

    def send(source, target, ss, rs, device):
        return pltpu.make_async_remote_copy(
            src_ref=source, dst_ref=target, send_sem=ss, recv_sem=rs, device_id=(device, gy), device_id_type=MESH)

    def matrix_to(k):
        peer = lax.rem(a + k, GROUP)
        return send(am_send.at[peer], am_recv.at[a], am_ss.at[peer], am_rs.at[a], base + peer)

    def source_to(k):
        peer = lax.rem(a + k, GROUP)
        return send(as_send.at[peer], as_recv.at[a], as_ss.at[peer], as_rs.at[a], base + peer)

    p_v[:, pl.ds(rows_y, 8), :] = jnp.zeros((cells, 8, lanes), jnp.float32)

    def first_loop(k, _):
        peer = lax.rem(a + k, GROUP)
        first_pass(peer, am_send.at[peer])
        matrix_to(k).start()
        return 0

    lax.fori_loop(1, GROUP, first_loop, 0)
    first_pass(a, am_recv.at[a])

    pltpu.make_async_copy(vzn_v, vz_out, out_sem.at[0]).start()

    for copy in edges:
        copy.wait()

    @pl.when(has_below)
    def _():
        for copy in ups:
            copy.wait_recv()

    @pl.when(has_above)
    def _():
        goes_down.wait_recv()

    own_damping = 1.0 / (1.0 + look_up(edge_mat[...], table))
    above = jnp.where(has_above, halo[2], 0.0)
    last_row = own_damping * (edge[1] - 0.5 * (above - edge[0]))
    below_damping = 1.0 / (1.0 + look_up(halo_mat[...], table))
    below_row = below_damping * (halo[1] - 0.5 * (edge[2] - halo[0]))
    below_row = jnp.where(has_below, below_row, 0.0)
    vyn_v[:, pl.ds(rows_y + 7, 1), :] = last_row
    vyn_v[:, pl.ds(7, 1), :] = below_row
    pltpu.make_async_copy(vyn_v.at[:, pl.ds(8, rows_y), :], vy_out, out_sem.at[1]).start()

    def second_pass(index, source_ref):
        here = at_rows(index)
        behind = pl.ds(pl.multiple_of(index * rows_a, 8), 8)
        total = left_source = None
        for x in range(cells):
            vyn = vyn_v[x, pl.ds(pl.multiple_of(index * rows_a + 8, 8), rows_a), :]
            lower = pltpu.roll(vyn, 1, axis=0)
            lower = jnp.where(row_of == 0, vyn_v[x, behind, :][7:8, :], lower)
            vzn = vzn_v[x, here, :]
            before = jnp.where(lane_of == 0, 0.0, pltpu.roll(vzn, 1, axis=1))
            source = (p_v[x, here, :] - 0.5 * (vyn - lower + vzn - before)) * scale
            total = source if x == 0 else source + passed
            if x < cells - 1:
                passed = total * r_v[x, here, :]
                tr_v[x, here, :] = passed
                share = total * a_v[x, here, :]
                left_source = share if x == 0 else left_source + share
        source_ref[0] = left_source
        source_ref[1] = total

    def second_loop(k, _):
        peer = lax.rem(a + k, GROUP)
        second_pass(peer, as_send.at[peer])
        source_to(k).start()
        return 0

    lax.fori_loop(1, GROUP, second_loop, 0)
    second_pass(a, as_recv.at[a])

    for stage in range(stages):
        pl.semaphore_wait(ring_sem.at[stage], len(ring))
        if stage + 1 < stages:
            for peer in ring:
                pl.semaphore_signal(ring_sem.at[stage + 1], inc=1, device_id=(peer, gy), device_id_type=MESH)

    def wait_a(k, _):
        peer = lax.rem(a + k, GROUP)
        send(am_send.at[peer], am_recv.at[peer], am_ss.at[peer], am_rs.at[peer], base + peer).wait()
        return 0

    lax.fori_loop(1, GROUP, wait_a, 0)
    segment, tree = build_matrix([tuple(am_recv[k, v] for v in range(3)) for k in range(GROUP)], 0, GROUP)
    for k in range(groups):
        for v in range(3):
            bm_send[k, v] = segment[v][rows_b * k:rows_b * (k + 1), :]
    bm_recv[z] = bm_send[z]

    def to_ring(k, source, target, ss, rs):
        peer = lax.rem(z + k, groups)
        return send(source.at[peer], target.at[z], ss.at[peer], rs.at[z], peer * GROUP + a)

    def from_ring(k, source, target, ss, rs):
        peer = lax.rem(z + k, groups)
        return send(source.at[peer], target.at[peer], ss.at[peer], rs.at[peer], peer * GROUP + a)

    for k in range(1, groups):
        to_ring(k, bm_send, bm_recv, bm_ss, bm_rs).start()

    def wait_as(k, _):
        peer = lax.rem(a + k, GROUP)
        send(as_send.at[peer], as_recv.at[peer], as_ss.at[peer], as_rs.at[peer], base + peer).wait()
        return 0

    lax.fori_loop(1, GROUP, wait_as, 0)
    levels = [None] * GROUP
    pair = build_source(tree, [(as_recv[k, 0], as_recv[k, 1]) for k in range(GROUP)], 0, GROUP, levels)
    for k in range(groups):
        for v in range(2):
            bs_send[k, v] = pair[v][rows_b * k:rows_b * (k + 1), :]
    bs_recv[z] = bs_send[z]
    for k in range(1, groups):
        to_ring(k, bs_send, bs_recv, bs_ss, bs_rs).start()

    for k in range(1, groups):
        from_ring(k, bm_send, bm_recv, bm_ss, bm_rs).wait()
    whole, tree_b = build_matrix([tuple(bm_recv[k, v] for v in range(3)) for k in range(groups)], 0, groups)
    end_inverse = 1.0 / (whole[0] + (whole[2] + 1.0))
    for k in range(1, groups):
        from_ring(k, bs_send, bs_recv, bs_ss, bs_rs).wait()
    levels_b = [None] * groups
    sums = build_source(tree_b, [(bs_recv[k, 0], bs_recv[k, 1]) for k in range(groups)], 0, groups, levels_b)
    values_b = [None] * groups
    nothing = jnp.zeros((rows_b, lanes), jnp.float32)
    values_b[groups - 1] = sums[1] * end_inverse
    spread(tree_b, levels_b, nothing, values_b[groups - 1], values_b)
    nodes_b[0] = nothing
    for k in range(groups):
        nodes_b[k + 1] = values_b[k]

    def back_b(k, slot):
        peer = lax.rem(z + k, groups)
        return send(nodes_b.at[pl.ds(peer, 2)], db_recv.at[slot(peer)], db_ss.at[peer], db_rs.at[slot(peer)],
                    peer * GROUP + a)

    for k in range(1, groups):
        back_b(k, lambda peer: z).start()
    db_recv[z] = nodes_b[pl.ds(z, 2)]
    for k in range(1, groups):
        back_b(k, lambda peer: peer).wait()
    before_all = jnp.concatenate([db_recv[k, 0] for k in range(groups)], axis=0)
    after_all = jnp.concatenate([db_recv[k, 1] for k in range(groups)], axis=0)
    values = [None] * GROUP
    values[GROUP - 1] = after_all
    spread(tree, levels, before_all, after_all, values)
    nodes_a[0] = before_all
    for k in range(GROUP):
        nodes_a[k + 1] = values[k]

    def back_a(k, owner):
        peer = lax.rem(a + k, GROUP)
        slot = owner(peer)
        return send(nodes_a.at[pl.ds(peer, 2)], da_recv.at[slot], da_ss.at[peer], da_rs.at[slot], base + peer)

    def back_loop(k, _):
        back_a(k, lambda peer: a).start()
        return 0

    lax.fori_loop(1, GROUP, back_loop, 0)

    def finish(index, before, after):
        here = at_rows(index)
        q_v[cells - 1, here, :] = after
        for x in range(cells - 2, -1, -1):
            after = tr_v[x, here, :] + r_v[x, here, :] * after + a_v[x, here, :] * before
            q_v[x, here, :] = after
        pltpu.make_async_copy(q_v.at[:, here, :], q_out.at[:, here, :], out_sem.at[2 + index]).start()

    finish(a, nodes_a[a], nodes_a[a + 1])

    def finish_loop(k, _):
        peer = lax.rem(a + GROUP - k, GROUP)
        send(nodes_a.at[pl.ds(peer, 2)], da_recv.at[peer], da_ss.at[peer], da_rs.at[peer], base + peer).wait()
        finish(peer, da_recv[peer, 0], da_recv[peer, 1])
        return 0

    lax.fori_loop(1, GROUP, finish_loop, 0)

    @pl.when(has_above)
    def _():
        for copy in ups:
            copy.wait_send()

    @pl.when(has_below)
    def _():
        goes_down.wait_send()

    pltpu.make_async_copy(vzn_v, vz_out, out_sem.at[0]).wait()
    pltpu.make_async_copy(vyn_v.at[:, pl.ds(8, rows_y), :], vy_out, out_sem.at[1]).wait()

    def drain(k, _):
        here = at_rows(k)
        pltpu.make_async_copy(q_v.at[:, here, :], q_out.at[:, here, :], out_sem.at[2 + k]).wait()
        return 0

    lax.fori_loop(0, GROUP, drain, 0)


def solution(mesh):
    groups = mesh.shape["gx"] // GROUP
    columns = mesh.shape["gy"]

    def body(pressure, vel_y, vel_z, material, absorb_table):
        cells, rows_y, lanes = pressure.shape
        rows_a = rows_y // GROUP
        rows_b = rows_a // groups
        f32 = jnp.float32
        vmem = pltpu.VMEM
        dma = pltpu.SemaphoreType.DMA
        scratch = [
            vmem((cells, rows_y + 8, lanes), f32),
            vmem((cells, rows_y, lanes), f32),
            vmem((cells, rows_y, lanes), f32),
            vmem((cells, rows_y, lanes), jnp.int32),
            vmem((cells, rows_y + 8, lanes), f32),
            vmem((cells, rows_y, lanes), f32),
            vmem((cells - 1, rows_y, lanes), f32),
            vmem((cells - 1, rows_y, lanes), f32),
            vmem((cells - 1, rows_y, lanes), f32),
            vmem((8, lanes), f32),
            vmem((cells, rows_y, lanes), f32),
            vmem((3, cells, 1, lanes), f32),
            vmem((cells, 1, lanes), jnp.int32),
            vmem((3, cells, 1, lanes), f32),
            vmem((cells, 1, lanes), jnp.int32),
            vmem((GROUP, 3, rows_a, lanes), f32),
            vmem((GROUP, 3, rows_a, lanes), f32),
            vmem((GROUP, 2, rows_a, lanes), f32),
            vmem((GROUP, 2, rows_a, lanes), f32),
            vmem((groups, 3, rows_b, lanes), f32),
            vmem((groups, 3, rows_b, lanes), f32),
            vmem((groups, 2, rows_b, lanes), f32),
            vmem((groups, 2, rows_b, lanes), f32),
            vmem((groups + 1, rows_b, lanes), f32),
            vmem((groups, 2, rows_b, lanes), f32),
            vmem((GROUP + 1, rows_a, lanes), f32),
            vmem((GROUP, 2, rows_a, lanes), f32),
            dma((4,)), dma((4,)), dma((2 + GROUP,)), dma((4,)), dma((4,)),
            dma((GROUP,)), dma((GROUP,)), dma((GROUP,)), dma((GROUP,)),
            dma((groups,)), dma((groups,)), dma((groups,)), dma((groups,)),
            dma((groups,)), dma((groups,)), dma((GROUP,)), dma((GROUP,)),
            pltpu.SemaphoreType.REGULAR((max(1, groups // 2 - 1),)),
        ]
        anywhere = pl.BlockSpec(memory_space=pltpu.HBM)
        return pl.pallas_call(
            functools.partial(kernel, groups, columns),
            out_shape=[jax.ShapeDtypeStruct(pressure.shape, f32)] * 3,
            in_specs=[pl.BlockSpec(memory_space=pltpu.SMEM)] + [anywhere] * 4,
            out_specs=[anywhere] * 3,
            scratch_shapes=scratch,
            compiler_params=pltpu.CompilerParams(collective_id=0, has_side_effects=True, vmem_limit_bytes=40 * 1024 * 1024),
            name="acoustic_step",
        )(absorb_table, pressure, vel_y, vel_z, material)

    return jax.shard_map(
        body,
        mesh=mesh,
        in_specs=(P("gx", "gy", None), P("gx", "gy", None), P("gx", "gy", None), P("gx", "gy", None), P()),
        out_specs=(P("gx", "gy", None), P("gx", "gy", None), P("gx", "gy", None)),
        check_vma=False,
    )
```

```python
import functools

import jax
import jax.numpy as jnp
from jax import lax
from jax.experimental import pallas as pl
from jax.experimental.pallas import tpu as pltpu
from jax.sharding import PartitionSpec as P

MATS = 8
RX = 65536
GROUP = 8
MESH = pl.DeviceIdType.MESH
LIMIT1 = 60 * 1024 * 1024
LIMIT2 = 8 * 1024 * 1024


def look_up(material, table):
    low = (material & 1) == 1
    mid = (material & 2) == 2
    high = material >= 4
    pairs = [jnp.where(low, table[2 * k + 1], table[2 * k]) for k in range(4)]
    quads = [jnp.where(mid, pairs[1], pairs[0]), jnp.where(mid, pairs[3], pairs[2])]
    return jnp.where(high, quads[1], quads[0])


def merge_matrix(left, right):
    ground = left[2] + right[1]
    inverse = 1.0 / (left[0] + right[0] + ground)
    to_left = left[0] * inverse
    to_right = right[0] * inverse
    joined = (to_left * right[0], left[1] + to_left * ground, right[2] + to_right * ground)
    return joined, (inverse, to_left, to_right)


def build_matrix(segments, low, high):
    if high - low == 1:
        return segments[low], None
    mid = (low + high) // 2
    left, left_tree = build_matrix(segments, low, mid)
    right, right_tree = build_matrix(segments, mid, high)
    joined, weights = merge_matrix(left, right)
    return joined, (mid - 1, weights, left_tree, right_tree)


def build_source(tree, sources, low, high, levels):
    if tree is None:
        return sources[low]
    node, (inverse, to_left, to_right), left_tree, right_tree = tree
    left = build_source(left_tree, sources, low, node + 1, levels)
    right = build_source(right_tree, sources, node + 1, high, levels)
    source = left[1] + right[0]
    levels[node] = source * inverse
    return left[0] + to_left * source, right[1] + to_right * source


def spread(tree, levels, before, after, values):
    if tree is None:
        return
    node, (_, to_left, to_right), left_tree, right_tree = tree
    value = levels[node] + to_left * before + to_right * after
    values[node] = value
    spread(left_tree, levels, before, value, values)
    spread(right_tree, levels, value, after, values)


def kernel(groups, columns, table_ref, p_hbm, vy_hbm, vz_hbm, mat_hbm,
           vyn_v, vzn_v, r_v, a_v, tr_v, ends_v,
           p_v, vy_v, vz_v, mat_v,
           edge, edge_mat, halo, halo_mat,
           am_send, am_recv, as_send, as_recv, bm_send, bm_recv, bs_send, bs_recv,
           nodes_b, db_recv, nodes_a, da_recv,
           in_sem, edge_sem, halo_send, halo_recv,
           am_ss, am_rs, as_ss, as_rs, bm_ss, bm_rs, bs_ss, bs_rs, db_ss, db_rs, da_ss, da_rs, ring_sem):
    cells, rows_y, lanes = vy_v.shape
    rows_a = rows_y // GROUP
    rows_b = rows_a // groups
    gx = lax.axis_index("gx")
    gy = lax.axis_index("gy")
    z = gx // GROUP
    a = gx % GROUP
    base = z * GROUP
    up = lax.rem(z + 1, groups) * GROUP + a
    down = lax.rem(z + groups - 1, groups) * GROUP + a
    ring = (up,) if groups == 2 else (up, down)
    has_above = gy < columns - 1
    has_below = gy > 0

    loads = [
        pltpu.make_async_copy(mat_hbm, mat_v, in_sem.at[0]),
        pltpu.make_async_copy(p_hbm, p_v.at[:, 0:rows_y, :], in_sem.at[1]),
        pltpu.make_async_copy(vy_hbm, vy_v, in_sem.at[2]),
        pltpu.make_async_copy(vz_hbm, vz_v, in_sem.at[3]),
    ]

    barrier = pltpu.get_barrier_semaphore()
    for k in range(1, GROUP):
        pl.semaphore_signal(barrier, inc=1, device_id=(base + lax.rem(a + k, GROUP), gy), device_id_type=MESH)
    for peer in ring:
        pl.semaphore_signal(barrier, inc=1, device_id=(peer, gy), device_id_type=MESH)

    @pl.when(has_above)
    def _():
        pl.semaphore_signal(barrier, inc=1, device_id=(gx, gy + 1), device_id_type=MESH)

    @pl.when(has_below)
    def _():
        pl.semaphore_signal(barrier, inc=1, device_id=(gx, gy - 1), device_id_type=MESH)

    for copy in loads:
        copy.start()
    last = pl.ds(rows_y - 1, 1)
    first = pl.ds(0, 1)
    edges = [
        pltpu.make_async_copy(mat_hbm.at[:, last, :], edge_mat, edge_sem.at[0]),
        pltpu.make_async_copy(p_hbm.at[:, last, :], edge.at[0], edge_sem.at[1]),
        pltpu.make_async_copy(vy_hbm.at[:, last, :], edge.at[1], edge_sem.at[2]),
        pltpu.make_async_copy(p_hbm.at[:, first, :], edge.at[2], edge_sem.at[3]),
    ]
    for copy in edges:
        copy.start()

    pl.semaphore_wait(barrier, GROUP - 1 + len(ring) + has_above.astype(jnp.int32) + has_below.astype(jnp.int32))

    def halo_up(k, source, target):
        return pltpu.make_async_remote_copy(
            src_ref=source, dst_ref=target, send_sem=halo_send.at[k], recv_sem=halo_recv.at[k],
            device_id=(gx, gy + 1), device_id_type=MESH)

    ups = [
        halo_up(0, mat_hbm.at[:, last, :], halo_mat),
        halo_up(1, p_hbm.at[:, last, :], halo.at[0]),
        halo_up(2, vy_hbm.at[:, last, :], halo.at[1]),
    ]
    goes_down = pltpu.make_async_remote_copy(
        src_ref=p_hbm.at[:, first, :], dst_ref=halo.at[2], send_sem=halo_send.at[3], recv_sem=halo_recv.at[3],
        device_id=(gx, gy - 1), device_id_type=MESH)

    @pl.when(has_above)
    def _():
        for copy in ups:
            copy.start()

    @pl.when(has_below)
    def _():
        goes_down.start()

    stages = groups // 2 - 1
    for stage in range(stages):
        for peer in ring:
            if stage == 0:
                pl.semaphore_signal(ring_sem.at[0], inc=1, device_id=(peer, gy), device_id_type=MESH)

    table = [table_ref[k] for k in range(MATS)]
    scale = 1.0 / RX

    loads[0].wait()
    loads[1].wait()
    loads[2].wait()
    loads[3].wait()
    row_of = lax.broadcasted_iota(jnp.int32, (rows_a, lanes), 0)
    lane_of = lax.broadcasted_iota(jnp.int32, (rows_a, lanes), 1)

    def at_rows(index, offset=0):
        return pl.ds(pl.multiple_of(index * rows_a + offset, 8), rows_a)

    def first_pass(index, matrix_ref):
        here = at_rows(index)
        after = pl.ds(pl.multiple_of(index * rows_a + rows_a, 8), 8)
        conductance = left_ground = carried = None
        for x in range(cells):
            weight = 1.0 + look_up(mat_v[x, here, :], table)
            damping = 1.0 / weight
            excess = weight * scale
            pressure = p_v[x, here, :]
            upper = pltpu.roll(pressure, rows_a - 1, axis=0)
            upper = jnp.where(row_of == rows_a - 1, p_v[x, after, :][0:1, :], upper)
            vyn_v[x, pl.ds(pl.multiple_of(index * rows_a + 8, 8), rows_a), :] = damping * (
                vy_v[x, here, :] - 0.5 * (upper - pressure))
            beyond = jnp.where(lane_of == lanes - 1, 0.0, pltpu.roll(pressure, lanes - 1, axis=1))
            vzn_v[x, here, :] = damping * (vz_v[x, here, :] - 0.5 * (beyond - pressure))
            if x == 0:
                ground = excess
                inverse = 1.0 / (2.0 + ground)
                conductance = inverse
                left_ground = conductance * ground
            elif x < cells - 1:
                ground = excess + carried
                inverse = 1.0 / (conductance + 1.0 + ground)
                conductance = conductance * inverse
                left_ground = left_ground + conductance * ground
            else:
                ground = excess + carried
            if x < cells - 1:
                carried = ground * inverse
                r_v[x, here, :] = inverse
                a_v[x, here, :] = conductance
        matrix_ref[0] = conductance
        matrix_ref[1] = left_ground
        matrix_ref[2] = ground

    def send(source, target, ss, rs, device):
        return pltpu.make_async_remote_copy(
            src_ref=source, dst_ref=target, send_sem=ss, recv_sem=rs, device_id=(device, gy), device_id_type=MESH)

    def matrix_to(k):
        peer = lax.rem(a + k, GROUP)
        return send(am_send.at[peer], am_recv.at[a], am_ss.at[peer], am_rs.at[a], base + peer)

    def source_to(k):
        peer = lax.rem(a + k, GROUP)
        return send(as_send.at[peer], as_recv.at[a], as_ss.at[peer], as_rs.at[a], base + peer)

    p_v[:, pl.ds(rows_y, 8), :] = jnp.zeros((cells, 8, lanes), jnp.float32)

    def first_loop(k, _):
        peer = lax.rem(a + k, GROUP)
        first_pass(peer, am_send.at[peer])
        matrix_to(k).start()
        return 0

    lax.fori_loop(1, GROUP, first_loop, 0)
    first_pass(a, am_recv.at[a])

    for copy in edges:
        copy.wait()

    @pl.when(has_below)
    def _():
        for copy in ups:
            copy.wait_recv()

    @pl.when(has_above)
    def _():
        goes_down.wait_recv()

    own_damping = 1.0 / (1.0 + look_up(edge_mat[...], table))
    above = jnp.where(has_above, halo[2], 0.0)
    last_row = own_damping * (edge[1] - 0.5 * (above - edge[0]))
    below_damping = 1.0 / (1.0 + look_up(halo_mat[...], table))
    below_row = below_damping * (halo[1] - 0.5 * (edge[2] - halo[0]))
    below_row = jnp.where(has_below, below_row, 0.0)
    vyn_v[:, pl.ds(rows_y + 7, 1), :] = last_row
    vyn_v[:, pl.ds(7, 1), :] = below_row

    def second_pass(index, source_ref):
        here = at_rows(index)
        behind = pl.ds(pl.multiple_of(index * rows_a, 8), 8)
        total = left_source = None
        for x in range(cells):
            vyn = vyn_v[x, pl.ds(pl.multiple_of(index * rows_a + 8, 8), rows_a), :]
            lower = pltpu.roll(vyn, 1, axis=0)
            lower = jnp.where(row_of == 0, vyn_v[x, behind, :][7:8, :], lower)
            vzn = vzn_v[x, here, :]
            before = jnp.where(lane_of == 0, 0.0, pltpu.roll(vzn, 1, axis=1))
            source = (p_v[x, here, :] - 0.5 * (vyn - lower + vzn - before)) * scale
            total = source if x == 0 else source + passed
            if x < cells - 1:
                passed = total * r_v[x, here, :]
                tr_v[x, here, :] = passed
                share = total * a_v[x, here, :]
                left_source = share if x == 0 else left_source + share
        source_ref[0] = left_source
        source_ref[1] = total

    def second_loop(k, _):
        peer = lax.rem(a + k, GROUP)
        second_pass(peer, as_send.at[peer])
        source_to(k).start()
        return 0

    lax.fori_loop(1, GROUP, second_loop, 0)
    second_pass(a, as_recv.at[a])

    for stage in range(stages):
        pl.semaphore_wait(ring_sem.at[stage], len(ring))
        if stage + 1 < stages:
            for peer in ring:
                pl.semaphore_signal(ring_sem.at[stage + 1], inc=1, device_id=(peer, gy), device_id_type=MESH)

    def wait_a(k, _):
        peer = lax.rem(a + k, GROUP)
        send(am_send.at[peer], am_recv.at[peer], am_ss.at[peer], am_rs.at[peer], base + peer).wait()
        return 0

    lax.fori_loop(1, GROUP, wait_a, 0)
    segment, tree = build_matrix([tuple(am_recv[k, v] for v in range(3)) for k in range(GROUP)], 0, GROUP)
    for k in range(groups):
        for v in range(3):
            bm_send[k, v] = segment[v][rows_b * k:rows_b * (k + 1), :]
    bm_recv[z] = bm_send[z]

    def to_ring(k, source, target, ss, rs):
        peer = lax.rem(z + k, groups)
        return send(source.at[peer], target.at[z], ss.at[peer], rs.at[z], peer * GROUP + a)

    def from_ring(k, source, target, ss, rs):
        peer = lax.rem(z + k, groups)
        return send(source.at[peer], target.at[peer], ss.at[peer], rs.at[peer], peer * GROUP + a)

    for k in range(1, groups):
        to_ring(k, bm_send, bm_recv, bm_ss, bm_rs).start()

    def wait_as(k, _):
        peer = lax.rem(a + k, GROUP)
        send(as_send.at[peer], as_recv.at[peer], as_ss.at[peer], as_rs.at[peer], base + peer).wait()
        return 0

    lax.fori_loop(1, GROUP, wait_as, 0)
    levels = [None] * GROUP
    pair = build_source(tree, [(as_recv[k, 0], as_recv[k, 1]) for k in range(GROUP)], 0, GROUP, levels)
    for k in range(groups):
        for v in range(2):
            bs_send[k, v] = pair[v][rows_b * k:rows_b * (k + 1), :]
    bs_recv[z] = bs_send[z]
    for k in range(1, groups):
        to_ring(k, bs_send, bs_recv, bs_ss, bs_rs).start()

    for k in range(1, groups):
        from_ring(k, bm_send, bm_recv, bm_ss, bm_rs).wait()
    whole, tree_b = build_matrix([tuple(bm_recv[k, v] for v in range(3)) for k in range(groups)], 0, groups)
    end_inverse = 1.0 / (whole[0] + (whole[2] + 1.0))
    for k in range(1, groups):
        from_ring(k, bs_send, bs_recv, bs_ss, bs_rs).wait()
    levels_b = [None] * groups
    sums = build_source(tree_b, [(bs_recv[k, 0], bs_recv[k, 1]) for k in range(groups)], 0, groups, levels_b)
    values_b = [None] * groups
    nothing = jnp.zeros((rows_b, lanes), jnp.float32)
    values_b[groups - 1] = sums[1] * end_inverse
    spread(tree_b, levels_b, nothing, values_b[groups - 1], values_b)
    nodes_b[0] = nothing
    for k in range(groups):
        nodes_b[k + 1] = values_b[k]

    def back_b(k, slot):
        peer = lax.rem(z + k, groups)
        return send(nodes_b.at[pl.ds(peer, 2)], db_recv.at[slot(peer)], db_ss.at[peer], db_rs.at[slot(peer)],
                    peer * GROUP + a)

    for k in range(1, groups):
        back_b(k, lambda peer: z).start()
    db_recv[z] = nodes_b[pl.ds(z, 2)]
    for k in range(1, groups):
        back_b(k, lambda peer: peer).wait()
    before_all = jnp.concatenate([db_recv[k, 0] for k in range(groups)], axis=0)
    after_all = jnp.concatenate([db_recv[k, 1] for k in range(groups)], axis=0)
    values = [None] * GROUP
    values[GROUP - 1] = after_all
    spread(tree, levels, before_all, after_all, values)
    nodes_a[0] = before_all
    for k in range(GROUP):
        nodes_a[k + 1] = values[k]

    def back_a(k, owner):
        peer = lax.rem(a + k, GROUP)
        slot = owner(peer)
        return send(nodes_a.at[pl.ds(peer, 2)], da_recv.at[slot], da_ss.at[peer], da_rs.at[slot], base + peer)

    def back_loop(k, _):
        back_a(k, lambda peer: a).start()
        return 0

    lax.fori_loop(1, GROUP, back_loop, 0)

    ends_v[a, 0] = nodes_a[a]
    ends_v[a, 1] = nodes_a[a + 1]

    def back_wait(k, _):
        peer = lax.rem(a + GROUP - k, GROUP)
        send(nodes_a.at[pl.ds(peer, 2)], da_recv.at[peer], da_ss.at[peer], da_rs.at[peer], base + peer).wait()
        ends_v[peer] = da_recv[peer]
        return 0

    lax.fori_loop(1, GROUP, back_wait, 0)

    @pl.when(has_above)
    def _():
        for copy in ups:
            copy.wait_send()

    @pl.when(has_below)
    def _():
        goes_down.wait_send()


def finish(vyn_v, vzn_v, r_v, a_v, tr_v, ends_v, q_out, vy_out, vz_out, q_v, out_sem):
    cells, rows_y, _ = vzn_v.shape
    rows_a = rows_y // GROUP
    velocities = [
        pltpu.make_async_copy(vzn_v, vz_out, out_sem.at[0]),
        pltpu.make_async_copy(vyn_v.at[:, pl.ds(8, rows_y), :], vy_out, out_sem.at[1]),
    ]
    pressures = []
    for index in range(GROUP):
        here = pl.ds(index * rows_a, rows_a)
        before, after = ends_v[index, 0], ends_v[index, 1]
        q_v[cells - 1, here, :] = after
        for x in range(cells - 2, -1, -1):
            after = tr_v[x, here, :] + r_v[x, here, :] * after + a_v[x, here, :] * before
            q_v[x, here, :] = after
        pressures.append(pltpu.make_async_copy(q_v.at[:, here, :], q_out.at[:, here, :], out_sem.at[2 + index]))
        pressures[-1].start()
        if index == 0:
            for copy in velocities:
                copy.start()
    for copy in velocities + pressures:
        copy.wait()


def solution(mesh):
    groups = mesh.shape["gx"] // GROUP
    columns = mesh.shape["gy"]

    def body(pressure, vel_y, vel_z, material, absorb_table):
        cells, rows_y, lanes = pressure.shape
        rows_a = rows_y // GROUP
        rows_b = rows_a // groups
        f32 = jnp.float32
        vmem = pltpu.VMEM
        dma = pltpu.SemaphoreType.DMA
        kept = [
            vmem((cells, rows_y + 8, lanes), f32),
            vmem((cells, rows_y, lanes), f32),
            vmem((cells - 1, rows_y, lanes), f32),
            vmem((cells - 1, rows_y, lanes), f32),
            vmem((cells - 1, rows_y, lanes), f32),
            vmem((GROUP, 2, rows_a, lanes), f32),
        ]
        scratch = [
            vmem((cells, rows_y + 8, lanes), f32),
            vmem((cells, rows_y, lanes), f32),
            vmem((cells, rows_y, lanes), f32),
            vmem((cells, rows_y, lanes), jnp.int32),
            vmem((3, cells, 1, lanes), f32),
            vmem((cells, 1, lanes), jnp.int32),
            vmem((3, cells, 1, lanes), f32),
            vmem((cells, 1, lanes), jnp.int32),
            vmem((GROUP, 3, rows_a, lanes), f32),
            vmem((GROUP, 3, rows_a, lanes), f32),
            vmem((GROUP, 2, rows_a, lanes), f32),
            vmem((GROUP, 2, rows_a, lanes), f32),
            vmem((groups, 3, rows_b, lanes), f32),
            vmem((groups, 3, rows_b, lanes), f32),
            vmem((groups, 2, rows_b, lanes), f32),
            vmem((groups, 2, rows_b, lanes), f32),
            vmem((groups + 1, rows_b, lanes), f32),
            vmem((groups, 2, rows_b, lanes), f32),
            vmem((GROUP + 1, rows_a, lanes), f32),
            vmem((GROUP, 2, rows_a, lanes), f32),
            dma((4,)), dma((4,)), dma((4,)), dma((4,)),
            dma((GROUP,)), dma((GROUP,)), dma((GROUP,)), dma((GROUP,)),
            dma((groups,)), dma((groups,)), dma((groups,)), dma((groups,)),
            dma((groups,)), dma((groups,)), dma((GROUP,)), dma((GROUP,)),
            pltpu.SemaphoreType.REGULAR((max(1, groups // 2 - 1),)),
        ]
        hbm = pl.BlockSpec(memory_space=pltpu.HBM)
        local = pl.BlockSpec(memory_space=pltpu.VMEM)
        held = pl.pallas_call(
            functools.partial(kernel, groups, columns),
            out_shape=kept,
            in_specs=[pl.BlockSpec(memory_space=pltpu.SMEM)] + [hbm] * 4,
            out_specs=[local] * len(kept),
            scratch_shapes=scratch,
            compiler_params=pltpu.CompilerParams(collective_id=0, has_side_effects=True, vmem_limit_bytes=LIMIT1),
            name="exchange",
        )(absorb_table, pressure, vel_y, vel_z, material)
        return pl.pallas_call(
            finish,
            out_shape=[jax.ShapeDtypeStruct(pressure.shape, f32)] * 3,
            in_specs=[local] * len(kept),
            out_specs=[hbm] * 3,
            scratch_shapes=[vmem((cells, rows_y, lanes), f32), dma((2 + GROUP,))],
            compiler_params=pltpu.CompilerParams(vmem_limit_bytes=LIMIT2),
            name="finish",
        )(*held)

    return jax.shard_map(
        body,
        mesh=mesh,
        in_specs=(P("gx", "gy", None), P("gx", "gy", None), P("gx", "gy", None), P("gx", "gy", None), P()),
        out_specs=(P("gx", "gy", None), P("gx", "gy", None), P("gx", "gy", None)),
        check_vma=False,
    )
```

```python
import functools

import jax
import jax.numpy as jnp
from jax import lax
from jax.experimental import pallas as pl
from jax.experimental.pallas import tpu as pltpu
from jax.sharding import PartitionSpec as P

MATS = 8
RX = 65536
GROUP = 8
LIMIT1 = 60 * 1024 * 1024
LIMIT2 = 8 * 1024 * 1024
MESH = pl.DeviceIdType.MESH


def look_up(material, table):
    low = (material & 1) == 1
    mid = (material & 2) == 2
    high = material >= 4
    pairs = [jnp.where(low, table[2 * k + 1], table[2 * k]) for k in range(4)]
    quads = [jnp.where(mid, pairs[1], pairs[0]), jnp.where(mid, pairs[3], pairs[2])]
    return jnp.where(high, quads[1], quads[0])


def merge_matrix(left, right):
    ground = left[2] + right[1]
    inverse = 1.0 / (left[0] + right[0] + ground)
    to_left = left[0] * inverse
    to_right = right[0] * inverse
    joined = (to_left * right[0], left[1] + to_left * ground, right[2] + to_right * ground)
    return joined, (inverse, to_left, to_right)


def build_matrix(segments, low, high):
    if high - low == 1:
        return segments[low], None
    mid = (low + high) // 2
    left, left_tree = build_matrix(segments, low, mid)
    right, right_tree = build_matrix(segments, mid, high)
    joined, weights = merge_matrix(left, right)
    return joined, (mid - 1, weights, left_tree, right_tree)


def build_source(tree, sources, low, high, levels):
    if tree is None:
        return sources[low]
    node, (inverse, to_left, to_right), left_tree, right_tree = tree
    left = build_source(left_tree, sources, low, node + 1, levels)
    right = build_source(right_tree, sources, node + 1, high, levels)
    source = left[1] + right[0]
    levels[node] = source * inverse
    return left[0] + to_left * source, right[1] + to_right * source


def spread(tree, levels, before, after, values):
    if tree is None:
        return
    node, (_, to_left, to_right), left_tree, right_tree = tree
    value = levels[node] + to_left * before + to_right * after
    values[node] = value
    spread(left_tree, levels, before, value, values)
    spread(right_tree, levels, value, after, values)


def kernel(groups, columns, table_hbm, p_hbm, vy_hbm, vz_hbm, mat_hbm,
           vyn_v, vzn_v, q_v,
           table_ref, p_v, vy_v, vz_v, mat_v, d_v, r_v, a_v, tr_v,
           edge, edge_mat, halo, halo_mat,
           am_send, am_recv, as_send, as_recv, bm_send, bm_recv, bs_send, bs_recv,
           nodes_b, db_recv, nodes_a, da_recv,
           table_sem, in_sem, edge_sem, halo_send, halo_recv,
           am_ss, am_rs, as_ss, as_rs, bm_ss, bm_rs, bs_ss, bs_rs, db_ss, db_rs, da_ss, da_rs, x_token, z_token):
    cells, rows_y, lanes = vy_v.shape
    rows_a = rows_y // GROUP
    rows_b = rows_a // 2
    chips = GROUP // 2
    solver = groups - 2
    gx = lax.axis_index("gx")
    gy = lax.axis_index("gy")
    z = gx // GROUP
    a = gx % GROUP
    chip = a // 2
    core = a % 2
    base = z * GROUP
    has_above = gy < columns - 1
    has_below = gy > 0

    def member(dx, dc):
        return lax.rem(chip + dx, chips) * 2 + lax.rem(core + dc, 2)

    def at_z(step):
        return lax.rem(z + step + groups, groups) * GROUP + a

    def signal(semaphore, device_x, device_y=None):
        pl.semaphore_signal(semaphore, inc=1, device_id=(device_x, gy if device_y is None else device_y), device_id_type=MESH)

    table_copy = pltpu.make_async_copy(table_hbm, table_ref, table_sem)
    table_copy.start()

    barrier = pltpu.get_barrier_semaphore()
    beside = [] if chips == 1 else ([1] if chips == 2 else [1, chips - 1])
    ring = [1] if groups == 2 else [1, -1]

    @pl.when(has_above)
    def _():
        signal(barrier, gx, gy + 1)

    @pl.when(has_below)
    def _():
        signal(barrier, gx, gy - 1)

    for dx in beside:
        for dc in range(2):
            signal(barrier, base + member(dx, dc))
    signal(barrier, base + member(0, 1))
    for step in ring:
        signal(barrier, at_z(step))

    loads = [
        pltpu.make_async_copy(mat_hbm, mat_v, in_sem.at[0]),
        pltpu.make_async_copy(p_hbm, p_v.at[:, 0:rows_y, :], in_sem.at[1]),
        pltpu.make_async_copy(vy_hbm, vy_v, in_sem.at[2]),
        pltpu.make_async_copy(vz_hbm, vz_v, in_sem.at[3]),
    ]
    for copy in loads:
        copy.start()
    last = pl.ds(rows_y - 1, 1)
    first = pl.ds(0, 1)
    edges = [
        pltpu.make_async_copy(mat_hbm.at[:, last, :], edge_mat, edge_sem.at[0]),
        pltpu.make_async_copy(p_hbm.at[:, last, :], edge.at[0], edge_sem.at[1]),
        pltpu.make_async_copy(vy_hbm.at[:, last, :], edge.at[1], edge_sem.at[2]),
        pltpu.make_async_copy(p_hbm.at[:, first, :], edge.at[2], edge_sem.at[3]),
    ]
    for copy in edges:
        copy.start()
    p_v[:, pl.ds(rows_y, 8), :] = jnp.zeros((cells, 8, lanes), jnp.float32)

    near = 2 * len(beside) + 1 + len(ring)
    pl.semaphore_wait(barrier, near + has_above.astype(jnp.int32) + has_below.astype(jnp.int32))

    def halo_up(k, source, target):
        return pltpu.make_async_remote_copy(
            src_ref=source, dst_ref=target, send_sem=halo_send.at[k], recv_sem=halo_recv.at[k],
            device_id=(gx, gy + 1), device_id_type=MESH)

    ups = [
        halo_up(0, mat_hbm.at[:, last, :], halo_mat),
        halo_up(1, p_hbm.at[:, last, :], halo.at[0]),
        halo_up(2, vy_hbm.at[:, last, :], halo.at[1]),
    ]
    goes_down = pltpu.make_async_remote_copy(
        src_ref=p_hbm.at[:, first, :], dst_ref=halo.at[2], send_sem=halo_send.at[3], recv_sem=halo_recv.at[3],
        device_id=(gx, gy - 1), device_id_type=MESH)

    @pl.when(has_above)
    def _():
        for copy in ups:
            copy.start()

    @pl.when(has_below)
    def _():
        goes_down.start()

    if chips > 2:
        signal(x_token, base + member(chips - 1, 0))

    half = groups // 2
    if groups > 2:
        @pl.when(z == groups - 1)
        def _():
            signal(z_token, at_z(1))

        if solver > half:
            @pl.when(z == solver)
            def _():
                signal(z_token, at_z(-1))

    scale = 1.0 / RX
    row_of = lax.broadcasted_iota(jnp.int32, (rows_a, lanes), 0)
    lane_of = lax.broadcasted_iota(jnp.int32, (rows_a, lanes), 1)

    def at_rows(index, offset=0):
        return pl.ds(pl.multiple_of(index * rows_a + offset, 8), rows_a)

    def send(source, target, ss, rs, device):
        return pltpu.make_async_remote_copy(
            src_ref=source, dst_ref=target, send_sem=ss, recv_sem=rs, device_id=(device, gy), device_id_type=MESH)

    def for_far(visit):
        if chips > 2:
            def far(k, _):
                visit(member(2, k))
                return 0
            lax.fori_loop(0, 2, far, 0)

    def for_close(visit):
        if chips > 2:
            def close(k, _):
                visit(member(1 + 2 * (k % 2), k // 2))
                return 0
            lax.fori_loop(0, 4, close, 0)
        elif chips == 2:
            visit(member(1, 0))
            visit(member(1, 1))

    def for_peers(visit):
        for_far(visit)
        for_close(visit)
        visit(member(0, 1))

    def matrix_pass(index, matrix_ref):
        here = at_rows(index)
        for x in range(cells):
            weight = 1.0 + look_up(mat_v[x, here, :], table)
            d_v[x, here, :] = 1.0 / weight
            excess = weight * scale
            if x == 0:
                ground = excess
                inverse = 1.0 / (2.0 + ground)
                conductance = inverse
                left_ground = conductance * ground
            elif x < cells - 1:
                ground = excess + carried
                inverse = 1.0 / (conductance + 1.0 + ground)
                conductance = conductance * inverse
                left_ground = left_ground + conductance * ground
            else:
                ground = excess + carried
            if x < cells - 1:
                carried = ground * inverse
                r_v[x, here, :] = inverse
                a_v[x, here, :] = conductance
        matrix_ref[0] = conductance
        matrix_ref[1] = left_ground
        matrix_ref[2] = ground

    table_copy.wait()
    table = [table_ref[k] for k in range(MATS)]
    loads[0].wait()

    def matrix_visit(peer):
        matrix_pass(peer, am_send.at[peer])
        send(am_send.at[peer], am_recv.at[a], am_ss, am_rs, base + peer).start()

    for_close(matrix_visit)
    matrix_visit(member(0, 1))
    matrix_pass(a, am_recv.at[a])
    if chips > 2:
        pl.semaphore_wait(x_token, 1)
    for_far(matrix_visit)

    loads[1].wait()
    loads[2].wait()
    loads[3].wait()

    def velocity_pass(index, _):
        here = at_rows(index)
        after = pl.ds(pl.multiple_of(index * rows_a + rows_a, 8), 8)
        for x in range(cells):
            damping = d_v[x, here, :]
            pressure = p_v[x, here, :]
            upper = pltpu.roll(pressure, rows_a - 1, axis=0)
            upper = jnp.where(row_of == rows_a - 1, p_v[x, after, :][0:1, :], upper)
            vyn_v[x, pl.ds(pl.multiple_of(index * rows_a + 8, 8), rows_a), :] = damping * (
                vy_v[x, here, :] - 0.5 * (upper - pressure))
            beyond = jnp.where(lane_of == lanes - 1, 0.0, pltpu.roll(pressure, lanes - 1, axis=1))
            vzn_v[x, here, :] = damping * (vz_v[x, here, :] - 0.5 * (beyond - pressure))
        return 0

    lax.fori_loop(0, GROUP, velocity_pass, 0)

    for copy in edges:
        copy.wait()

    @pl.when(has_below)
    def _():
        for copy in ups:
            copy.wait_recv()

    @pl.when(has_above)
    def _():
        goes_down.wait_recv()

    own_damping = 1.0 / (1.0 + look_up(edge_mat[...], table))
    above = jnp.where(has_above, halo[2], 0.0)
    last_row = own_damping * (edge[1] - 0.5 * (above - edge[0]))
    below_damping = 1.0 / (1.0 + look_up(halo_mat[...], table))
    below_row = below_damping * (halo[1] - 0.5 * (edge[2] - halo[0]))
    below_row = jnp.where(has_below, below_row, 0.0)
    vyn_v[:, pl.ds(rows_y + 7, 1), :] = last_row
    vyn_v[:, pl.ds(7, 1), :] = below_row

    def source_pass(index, source_ref):
        here = at_rows(index)
        behind = pl.ds(pl.multiple_of(index * rows_a, 8), 8)
        for x in range(cells):
            vyn = vyn_v[x, pl.ds(pl.multiple_of(index * rows_a + 8, 8), rows_a), :]
            lower = pltpu.roll(vyn, 1, axis=0)
            lower = jnp.where(row_of == 0, vyn_v[x, behind, :][7:8, :], lower)
            vzn = vzn_v[x, here, :]
            before = jnp.where(lane_of == 0, 0.0, pltpu.roll(vzn, 1, axis=1))
            source = (p_v[x, here, :] - 0.5 * (vyn - lower + vzn - before)) * scale
            total = source if x == 0 else source + passed
            if x < cells - 1:
                passed = total * r_v[x, here, :]
                tr_v[x, here, :] = passed
                share = total * a_v[x, here, :]
                left_source = share if x == 0 else left_source + share
        source_ref[0] = left_source
        source_ref[1] = total

    def source_visit(peer):
        source_pass(peer, as_send.at[peer])
        send(as_send.at[peer], as_recv.at[a], as_ss, as_rs, base + peer).start()

    for_peers(source_visit)
    source_pass(a, as_recv.at[a])

    if groups > 2:
        @pl.when(z < solver)
        def _():
            pl.semaphore_wait(z_token, 1)

        @pl.when(z < min(half, solver) - 1)
        def _():
            signal(z_token, at_z(1))

        @pl.when((z > half) & (z < solver))
        def _():
            signal(z_token, at_z(-1))

    def to_solver(j, source, target, ss, rs):
        return send(source.at[j], target.at[z], ss, rs, (solver + j) * GROUP + a)

    def hand_up(source, target, ss, rs):
        for j in range(2):
            @pl.when(z != solver + j)
            def _():
                to_solver(j, source, target, ss, rs).start()

            @pl.when(z == solver + j)
            def _():
                target[z] = source[j]

    others = pl.ds(0, GROUP - 1)
    partner = base + member(0, 1)
    all_matrix = send(am_send.at[others], am_recv.at[others], am_ss, am_rs, partner)
    all_source = send(as_send.at[others], as_recv.at[others], as_ss, as_rs, partner)
    all_back = send(da_recv.at[others], da_recv.at[others], da_ss, da_rs.at[0], partner)
    all_matrix.wait_recv()
    segment, tree = build_matrix([tuple(am_recv[k, v] for v in range(3)) for k in range(GROUP)], 0, GROUP)
    for j in range(2):
        for v in range(3):
            bm_send[j, v] = segment[v][rows_b * j:rows_b * (j + 1), :]
    hand_up(bm_send, bm_recv, bm_ss, bm_rs)

    all_source.wait_recv()
    levels = [None] * GROUP
    pair = build_source(tree, [(as_recv[k, 0], as_recv[k, 1]) for k in range(GROUP)], 0, GROUP, levels)
    for j in range(2):
        for v in range(2):
            bs_send[j, v] = pair[v][rows_b * j:rows_b * (j + 1), :]
    hand_up(bs_send, bs_recv, bs_ss, bs_rs)

    def back_b(peer, j):
        return send(nodes_b.at[pl.ds(peer, 2)], db_recv.at[j], db_ss, db_rs.at[j], peer * GROUP + a)

    @pl.when(z >= solver)
    def _():
        j = z - solver
        every = pl.ds(0, groups - 1)
        send(bm_recv.at[every], bm_recv.at[every], bm_ss, bm_rs, at_z(1)).wait_recv()
        whole, tree_b = build_matrix([tuple(bm_recv[k, v] for v in range(3)) for k in range(groups)], 0, groups)
        end_inverse = 1.0 / (whole[0] + (whole[2] + 1.0))
        send(bs_recv.at[every], bs_recv.at[every], bs_ss, bs_rs, at_z(1)).wait_recv()
        levels_b = [None] * groups
        sums = build_source(tree_b, [(bs_recv[k, 0], bs_recv[k, 1]) for k in range(groups)], 0, groups, levels_b)
        values_b = [None] * groups
        nothing = jnp.zeros((rows_b, lanes), jnp.float32)
        values_b[groups - 1] = sums[1] * end_inverse
        spread(tree_b, levels_b, nothing, values_b[groups - 1], values_b)
        nodes_b[0] = nothing
        for k in range(groups):
            nodes_b[k + 1] = values_b[k]
        for k in range(1, groups):
            back_b(lax.rem(z + k, groups), j).start()
        db_recv[j] = nodes_b[pl.ds(z, 2)]

    for j in range(2):
        @pl.when(z != solver + j)
        def _():
            back_b(0, j).wait_recv()

    before_all = jnp.concatenate([db_recv[0, 0], db_recv[1, 0]], axis=0)
    after_all = jnp.concatenate([db_recv[0, 1], db_recv[1, 1]], axis=0)
    values = [None] * GROUP
    values[GROUP - 1] = after_all
    spread(tree, levels, before_all, after_all, values)
    nodes_a[0] = before_all
    for k in range(GROUP):
        nodes_a[k + 1] = values[k]

    def back_a(peer, slot):
        return send(nodes_a.at[pl.ds(peer, 2)], da_recv.at[slot], da_ss, da_rs.at[slot], base + peer)

    def back_start(peer):
        back_a(peer, a).start()

    for_peers(back_start)

    def finish_lines(index, before, after):
        here = at_rows(index)
        q_v[cells - 1, here, :] = after
        for x in range(cells - 2, -1, -1):
            after = tr_v[x, here, :] + r_v[x, here, :] * after + a_v[x, here, :] * before
            q_v[x, here, :] = after

    finish_lines(a, nodes_a[a], nodes_a[a + 1])

    def back_wait(peer):
        back_a(peer, peer).wait_recv()
        finish_lines(peer, da_recv[peer, 0], da_recv[peer, 1])

    back_wait(member(0, 1))
    if chips > 2:
        def close_wait(k, _):
            back_wait(member(1 + 2 * (k % 2), k // 2))
            return 0
        lax.fori_loop(0, 4, close_wait, 0)

        def far_wait(k, _):
            back_wait(member(2, k))
            return 0
        lax.fori_loop(0, 2, far_wait, 0)
    elif chips == 2:
        back_wait(member(1, 0))
        back_wait(member(1, 1))

    @pl.when(has_above)
    def _():
        for copy in ups:
            copy.wait_send()

    @pl.when(has_below)
    def _():
        goes_down.wait_send()

    all_matrix.wait_send()
    all_source.wait_send()
    all_back.wait_send()

    @pl.when(z < solver)
    def _():
        send(bm_send, bm_recv.at[pl.ds(0, 2)], bm_ss, bm_rs, at_z(1)).wait_send()
        send(bs_send, bs_recv.at[pl.ds(0, 2)], bs_ss, bs_rs, at_z(1)).wait_send()

    @pl.when(z >= solver)
    def _():
        every = pl.ds(0, groups - 1)
        send(bm_send.at[0], bm_recv.at[0], bm_ss, bm_rs, at_z(1)).wait_send()
        send(bs_send.at[0], bs_recv.at[0], bs_ss, bs_rs, at_z(1)).wait_send()
        send(bs_recv.at[every], bs_recv.at[every], db_ss, bs_rs, at_z(1)).wait_send()


def finish(vyn_v, vzn_v, q_v, q_out, vy_out, vz_out, out_sem):
    rows_y = vzn_v.shape[1]
    copies = [
        pltpu.make_async_copy(q_v, q_out, out_sem.at[0]),
        pltpu.make_async_copy(vzn_v, vz_out, out_sem.at[1]),
        pltpu.make_async_copy(vyn_v.at[:, pl.ds(8, rows_y), :], vy_out, out_sem.at[2]),
    ]
    for copy in copies:
        copy.start()
    for copy in copies:
        copy.wait()


def solution(mesh):
    groups = mesh.shape["gx"] // GROUP
    columns = mesh.shape["gy"]

    def body(pressure, vel_y, vel_z, material, absorb_table):
        cells, rows_y, lanes = pressure.shape
        rows_a = rows_y // GROUP
        rows_b = rows_a // 2
        f32 = jnp.float32
        vmem = pltpu.VMEM
        dma = pltpu.SemaphoreType.DMA
        kept = [
            vmem((cells, rows_y + 8, lanes), f32),
            vmem((cells, rows_y, lanes), f32),
            vmem((cells, rows_y, lanes), f32),
        ]
        scratch = [
            pltpu.SMEM((MATS,), f32),
            vmem((cells, rows_y + 8, lanes), f32),
            vmem((cells, rows_y, lanes), f32),
            vmem((cells, rows_y, lanes), f32),
            vmem((cells, rows_y, lanes), jnp.int32),
            vmem((cells, rows_y, lanes), f32),
            vmem((cells - 1, rows_y, lanes), f32),
            vmem((cells - 1, rows_y, lanes), f32),
            vmem((cells - 1, rows_y, lanes), f32),
            vmem((3, cells, 1, lanes), f32),
            vmem((cells, 1, lanes), jnp.int32),
            vmem((3, cells, 1, lanes), f32),
            vmem((cells, 1, lanes), jnp.int32),
            vmem((GROUP, 3, rows_a, lanes), f32),
            vmem((GROUP, 3, rows_a, lanes), f32),
            vmem((GROUP, 2, rows_a, lanes), f32),
            vmem((GROUP, 2, rows_a, lanes), f32),
            vmem((2, 3, rows_b, lanes), f32),
            vmem((groups, 3, rows_b, lanes), f32),
            vmem((2, 2, rows_b, lanes), f32),
            vmem((groups, 2, rows_b, lanes), f32),
            vmem((groups + 1, rows_b, lanes), f32),
            vmem((2, 2, rows_b, lanes), f32),
            vmem((GROUP + 1, rows_a, lanes), f32),
            vmem((GROUP, 2, rows_a, lanes), f32),
            dma, dma((4,)), dma((4,)), dma((4,)), dma((4,)),
            dma, dma, dma, dma,
            dma, dma, dma, dma,
            dma, dma((2,)), dma, dma((GROUP,)),
            pltpu.SemaphoreType.REGULAR, pltpu.SemaphoreType.REGULAR,
        ]
        hbm = pl.BlockSpec(memory_space=pltpu.HBM)
        local = pl.BlockSpec(memory_space=pltpu.VMEM)
        held = pl.pallas_call(
            functools.partial(kernel, groups, columns),
            out_shape=kept,
            in_specs=[hbm] * 5,
            out_specs=[local] * len(kept),
            scratch_shapes=scratch,
            compiler_params=pltpu.CompilerParams(collective_id=0, has_side_effects=True, vmem_limit_bytes=LIMIT1),
            name="exchange",
        )(absorb_table, pressure, vel_y, vel_z, material)
        return pl.pallas_call(
            finish,
            out_shape=[jax.ShapeDtypeStruct(pressure.shape, f32)] * 3,
            in_specs=[local] * len(kept),
            out_specs=[hbm] * 3,
            scratch_shapes=[dma((3,))],
            compiler_params=pltpu.CompilerParams(vmem_limit_bytes=LIMIT2),
            name="finish",
        )(*held)

    return jax.shard_map(
        body,
        mesh=mesh,
        in_specs=(P("gx", "gy", None), P("gx", "gy", None), P("gx", "gy", None), P("gx", "gy", None), P()),
        out_specs=(P("gx", "gy", None), P("gx", "gy", None), P("gx", "gy", None)),
        check_vma=False,
    )
```
